32 devices in a mesh: batch: 2 (over x), blk: 16 (over z, y, core).
Axes of the slice: x: 2, y: 2, z: 4, core: 2. Of those that a mesh axis runs over, the one named last changes fastest.
Arguments:
- stream: bfloat16 [32768, 1024], P(('batch', 'blk')), parts along dimension 0, may hold values from -6 to 6
- norm_gain: float32 [4, 1024], replicated, may hold values from 0.1 to 1.9
- norm_bias: float32 [4, 1024], replicated, may hold values from -3 to 3
- proj_in: bfloat16 [4, 1024, 512], replicated, may hold values from -0.1875 to 0.1875
- convolution_taps: bfloat16 [4, 3, 512, 512], replicated, may hold values from -0.15625 to 0.15625
- output_projection: bfloat16 [4, 512, 1024], replicated, may hold values from -0.25 to 0.25
Outputs:
- result: bfloat16 [32768, 1024], P(('batch', 'blk')), parts along dimension 0
The draws below stay inside these ranges and needn't reach their ends.
There are 2 independent parts, one for each index of `batch`. The reference program is written for one: setup_inputs(seed, part) draws one part's arguments, and reference() takes and returns one part's arrays. A program takes and returns all parts, laid end to end along the dimension named above; an argument that names none is the same for every part. Nothing has to cross between parts.
All inputs are finite; a program needn't handle non-finite values.
Results may differ from the reference program's by a relative error of at most 0.017.
Values may be sent and summed in bfloat16 or wider, within the bound.
No kernel may reach another device: no remote copies, remote signals or barrier semaphores. Data moves between devices by JAX's collectives and lax.ppermute only.
A program may use at most 64 MiB of HBM per device.

```python
import jax
import jax.numpy as jnp
from jax import lax

D = 1024
H = 512
LAYERS = 4
DILATION_START = 512
SEQ = 16384


def block_levels(rng, dims, pieces, least, high):
    def one(position, parts):
        steps = jax.random.uniform(jax.random.fold_in(jax.random.fold_in(rng, 6), position), (parts,), jnp.float32, least / len(pieces), high / len(pieces))
        return jnp.repeat(jnp.exp(steps), dims[position] // parts).reshape((-1,) + (1,) * (len(dims) - position - 1))

    factor_of = one(*pieces[0])
    for cut in pieces[1:]:
        factor_of = factor_of * one(*cut)
    return factor_of


def scatter_about(stream_key, dims, deviation, limit, split=(), dtype=jnp.bfloat16):
    array = jax.random.normal(stream_key, dims, jnp.float32) * deviation
    if len(split) > 0:
        array = block_levels(stream_key, dims, split, -0.22, 0.18) * array
    return jnp.clip(array, min=-limit, max=limit).astype(dtype)


def setup_inputs(seed: int = 0, part: int = 0) -> dict:
    keys = jax.random.split(jax.random.key(seed), 7)
    part_splits = jax.random.split(jax.random.fold_in(keys[6], part), 7)
    stream = scatter_about(part_splits[0], (SEQ, D), 1.0, 6.0, ((0, 16),))
    norm_gain = jnp.clip(1.0 + 0.18 * jax.random.normal(keys[1], (LAYERS, D), jnp.float32), 0.1, 1.9)
    norm_bias = scatter_about(keys[2], (LAYERS, D), 0.5, 3.0, (), jnp.float32)
    proj_in = scatter_about(keys[3], (LAYERS, D, H), D ** -0.5, 0.1875)
    convolution_taps = scatter_about(keys[4], (LAYERS, 3, H, H), (3 * H) ** -0.5, 0.15625)
    output_projection = scatter_about(keys[5], (LAYERS, H, D), H ** -0.5, 0.25)
    return {"stream": stream, "norm_gain": norm_gain, "norm_bias": norm_bias, "proj_in": proj_in, "convolution_taps": convolution_taps, "output_projection": output_projection}


EPSILON = 1e-05

def normalize(stream, scales, offsets):
    values = stream.astype(jnp.float32)
    average = lax.optimization_barrier(jnp.mean(values, axis=1, keepdims=True))
    centred_values = values - average
    variance = lax.optimization_barrier(jnp.mean(centred_values * centred_values, axis=1, keepdims=True))
    return (centred_values * jax.lax.rsqrt(variance + EPSILON) * scales + offsets).astype(jnp.bfloat16)

def reference(stream, norm_gain, norm_bias, proj_in, convolution_taps, output_projection):
    for block_depth in range(LAYERS):
        dilation_factor = DILATION_START * 2 ** block_depth
        normed = normalize(stream, norm_gain[block_depth], norm_bias[block_depth])
        narrow = jnp.dot(normed, proj_in[block_depth], preferred_element_type=jnp.float32).astype(jnp.bfloat16)
        kernel = convolution_taps[block_depth]
        convolved = jnp.dot(jnp.roll(narrow, dilation_factor, axis=0), kernel[0], preferred_element_type=jnp.float32)
        convolved = convolved + jnp.dot(narrow, kernel[1], preferred_element_type=jnp.float32)
        convolved = convolved + jnp.dot(jnp.roll(narrow, -dilation_factor, axis=0), kernel[2], preferred_element_type=jnp.float32)
        activated = jax.nn.gelu(convolved, approximate=False).astype(jnp.bfloat16)
        update = jnp.dot(activated, output_projection[block_depth], preferred_element_type=jnp.float32)
        stream = (stream.astype(jnp.float32) + update).astype(jnp.bfloat16)
    return stream
```

```python
import functools

import jax
import jax.numpy as jnp
from jax import lax
from jax.experimental import pallas as pl
from jax.experimental.pallas import tpu as pltpu
from jax.sharding import PartitionSpec as P


DILATION_START = 512
EPSILON = 1e-05
CORES = 2
CHUNKS = 2
TILE = 256


VMEM = pl.BlockSpec(memory_space=pltpu.VMEM)
HBM = pl.BlockSpec(memory_space=pl.ANY)


def gelu(x):
    return 0.5 * x * (1.0 + lax.erf(x * (0.5**0.5)))


def project(x, gain, bias, proj):
    values = x.astype(jnp.float32)
    average = jnp.mean(values, axis=1, keepdims=True)
    centred = values - average
    variance = jnp.mean(centred * centred, axis=1, keepdims=True)
    normed = (centred * lax.rsqrt(variance + EPSILON) * gain + bias).astype(jnp.bfloat16)
    return jnp.dot(normed, proj, preferred_element_type=jnp.float32).astype(jnp.bfloat16)


def advance(x, earlier, middle, after, taps, output):
    convolved = jnp.dot(middle, taps[1], preferred_element_type=jnp.float32)
    convolved = convolved + jnp.dot(earlier, taps[0], preferred_element_type=jnp.float32)
    convolved = convolved + jnp.dot(after, taps[2], preferred_element_type=jnp.float32)
    activated = gelu(convolved).astype(jnp.bfloat16)
    update = jnp.dot(activated, output, preferred_element_type=jnp.float32)
    return (x.astype(jnp.float32) + update).astype(jnp.bfloat16)


def tiles(rows):
    size = min(TILE, rows)
    return [slice(r, r + size) for r in range(0, rows, size)]


def position():
    index = lax.axis_index("blk")
    return index // CORES, index % CORES


def start_all(copies):
    for copy in copies:
        copy.start()


def enter_kernel(chips, width, *refs):
    pieces, (gain, bias, proj_hbm, x_ref, narrow_ref, proj, sem) = refs[:chips], refs[chips:]
    copy = pltpu.make_async_copy(proj_hbm.at[0], proj, sem)
    copy.start()
    chip, _ = position()
    for k in range(chips):
        x_ref[pl.ds(pl.multiple_of((chip ^ k) * width, width), width), :] = pieces[k][...]
    copy.wait()
    for t in tiles(chips * width):
        narrow_ref[t, :] = project(x_ref[t, :], gain[0:1, :], bias[0:1, :], proj[...])


def load_partner(partner, padded, chips, width):
    rows = chips * width
    padded[pl.ds(width, rows), :] = partner[...]
    padded[pl.ds(0, width), :] = partner[pl.ds(rows - width, width), :]
    padded[pl.ds(width + rows, width), :] = partner[pl.ds(0, width), :]


def slot_kernel(chips, width, slots, block, x_in, narrow, partner, gain, bias, taps_hbm, output_hbm, proj_hbm,
                x_ref, narrow_ref, taps, output, proj, padded, earlier, after, sems):
    copies = [
        pltpu.make_async_copy(taps_hbm.at[block], taps, sems.at[0]),
        pltpu.make_async_copy(output_hbm.at[block], output, sems.at[1]),
        pltpu.make_async_copy(proj_hbm.at[block + 1], proj, sems.at[2]),
    ]
    start_all(copies)
    _, core = position()
    load_partner(partner, padded, chips, width)
    part = width // slots
    shift = 2**block
    for c in range(chips):
        for slot in range(slots):
            to = pl.ds(c * width + slot * part, part)
            if slot >= shift:
                earlier[to, :] = narrow[pl.ds(c * width + (slot - shift) * part, part), :]
            else:
                at = (c + core) * width + (slot - shift + slots) * part
                earlier[to, :] = padded[pl.ds(pl.multiple_of(at, part), part), :]
            if slot + shift < slots:
                after[to, :] = narrow[pl.ds(c * width + (slot + shift) * part, part), :]
            else:
                at = (c + core + 1) * width + (slot + shift - slots) * part
                after[to, :] = padded[pl.ds(pl.multiple_of(at, part), part), :]
    for copy in copies:
        copy.wait()
    for t in tiles(chips * width):
        x = advance(x_in[t, :], earlier[t, :], narrow[t, :], after[t, :], taps, output[...])
        x_ref[t, :] = x
        narrow_ref[t, :] = project(
            x, gain[block + 1 : block + 2, :], bias[block + 1 : block + 2, :], proj[...]
        )


def rest_kernel(chips, width, first, layers, x_in, narrow, partner, gain, bias, taps_hbm, output_hbm, proj_hbm, *refs):
    pieces, (taps, output, proj, padded, own, x_ref, sems) = refs[:chips], refs[chips:]
    blocks = range(first, layers)
    rows = chips * width
    copies = {}
    for n, block in enumerate(blocks):
        copies[block] = [
            pltpu.make_async_copy(taps_hbm.at[block], taps.at[n], sems.at[n, 0]),
            pltpu.make_async_copy(output_hbm.at[block], output.at[n], sems.at[n, 1]),
        ]
        if block + 1 < layers:
            copies[block].append(pltpu.make_async_copy(proj_hbm.at[block + 1], proj.at[n], sems.at[n, 2]))
        start_all(copies[block])
    chip, core = position()
    load_partner(partner, padded, chips, width)
    pad = (own.shape[1] - rows) // 2
    for n, block in enumerate(blocks):
        for copy in copies[block]:
            copy.wait()
        for t in tiles(rows):
            size = t.stop - t.start
            if n == 0:
                x = x_in[t, :]
                middle = narrow[t, :]
                earlier = padded[pl.ds(pl.multiple_of(core * width + t.start, width), size), :]
                after = padded[pl.ds(pl.multiple_of((core + 1) * width + t.start, width), size), :]
            else:
                x = x_ref[t, :]
                shift = 2 ** (n - 1) * width
                held = own.at[n - 1]
                middle = held[pl.ds(pad + t.start, size), :]
                earlier = held[pl.ds(pad + t.start - shift, size), :]
                after = held[pl.ds(pad + t.start + shift, size), :]
            x = advance(x, earlier, middle, after, taps.at[n], output[n])
            x_ref[t, :] = x
            if block + 1 < layers:
                own[n, pl.ds(pad + t.start, size), :] = project(
                    x, gain[block + 1 : block + 2, :], bias[block + 1 : block + 2, :], proj[n]
                )
        if block + 1 < layers:
            own[n, pl.ds(0, pad), :] = own[n, pl.ds(rows, pad), :]
            own[n, pl.ds(pad + rows, pad), :] = own[n, pl.ds(pad, pad), :]
    for k in range(chips):
        pieces[k][...] = x_ref[pl.ds(pl.multiple_of((chip ^ k) * width, width), width), :]


def estimate(rows, model, neck, blocks):
    return pl.CostEstimate(
        flops=2 * rows * blocks * (2 * model * neck + 3 * neck * neck),
        bytes_accessed=blocks * 2 * (2 * model * neck + 3 * neck * neck) + 8 * rows * model,
        transcendentals=0,
    )


def chunk_count(chips):
    return max(1, min(CHUNKS, DILATION_START // chips // 16))


def body(stream, norm_gain, norm_bias, proj_in, convolution_taps, output_projection):
    rows, model = stream.shape
    layers, neck = norm_gain.shape[0], proj_in.shape[2]
    peers = lax.axis_size("blk")
    chips = peers // CORES
    slots = rows // DILATION_START
    span = DILATION_START // chips
    chunks = chunk_count(chips)
    part = span // chunks
    width = slots * part
    count = chips * width
    bf16 = jnp.bfloat16
    chip = lax.axis_index("blk") // CORES

    def to_chip(piece, k):
        return lax.ppermute(piece, "blk", [(i, i ^ (k * CORES)) for i in range(peers)])

    def other_core(narrow):
        return lax.ppermute(narrow, "blk", [(i, i ^ 1) for i in range(peers)])

    shape = jax.ShapeDtypeStruct
    enter = pl.pallas_call(
        functools.partial(enter_kernel, chips, width),
        out_shape=(shape((count, model), bf16), shape((count, neck), bf16)),
        in_specs=[VMEM] * chips + [VMEM, VMEM, HBM],
        out_specs=(VMEM, VMEM),
        scratch_shapes=[pltpu.VMEM((model, neck), bf16), pltpu.SemaphoreType.DMA],
        cost_estimate=estimate(count, model, neck, 1),
        name="enter",
    )
    slot_block = pl.pallas_call(
        functools.partial(slot_kernel, chips, width, slots, 0),
        out_shape=(shape((count, model), bf16), shape((count, neck), bf16)),
        in_specs=[VMEM] * 5 + [HBM] * 3,
        out_specs=(VMEM, VMEM),
        scratch_shapes=[
            pltpu.VMEM((3, neck, neck), bf16),
            pltpu.VMEM((neck, model), bf16),
            pltpu.VMEM((model, neck), bf16),
            pltpu.VMEM((count + 2 * width, neck), bf16),
            pltpu.VMEM((count, neck), bf16),
            pltpu.VMEM((count, neck), bf16),
            pltpu.SemaphoreType.DMA((3,)),
        ],
        cost_estimate=estimate(count, model, neck, 1),
        name="slot_block",
    )
    held = layers - 1
    pad = 2 ** (held - 2) * width
    rest = pl.pallas_call(
        functools.partial(rest_kernel, chips, width, 1, layers),
        out_shape=tuple(shape((width, model), bf16) for _ in range(chips)),
        in_specs=[VMEM] * 5 + [HBM] * 3,
        out_specs=tuple(VMEM for _ in range(chips)),
        scratch_shapes=[
            pltpu.VMEM((held, 3, neck, neck), bf16),
            pltpu.VMEM((held, neck, model), bf16),
            pltpu.VMEM((held - 1, model, neck), bf16),
            pltpu.VMEM((count + 2 * width, neck), bf16),
            pltpu.VMEM((held - 1, count + 2 * pad, neck), bf16),
            pltpu.VMEM((count, model), bf16),
            pltpu.SemaphoreType.DMA((held, 3)),
        ],
        cost_estimate=estimate(count, model, neck, held),
        name="rest",
    )

    grid = stream.reshape(slots, chips * chunks, part, model)
    arrived = []
    for j in range(chunks):
        pieces = []
        for k in range(chips):
            piece = lax.dynamic_slice_in_dim(grid, (chip ^ k) * chunks + j, 1, axis=1).reshape(width, model)
            pieces.append(to_chip(piece, k) if k else piece)
        arrived.append(pieces)

    left = []
    for j in range(chunks):
        x, narrow = enter(*arrived[j], norm_gain, norm_bias, proj_in)
        weights = (norm_gain, norm_bias, convolution_taps, output_projection, proj_in)
        x, narrow = slot_block(x, narrow, other_core(narrow), *weights)
        partner = other_core(narrow)
        pieces = rest(x, narrow, partner, *weights)
        left.append([to_chip(piece, k) if k else piece for k, piece in enumerate(pieces)])

    result = jnp.zeros(grid.shape, bf16)
    for j in range(chunks):
        for k in range(chips):
            piece = left[j][k].reshape(slots, 1, part, model)
            result = lax.dynamic_update_slice_in_dim(result, piece, (chip ^ k) * chunks + j, axis=1)
    return result.reshape(rows, model)


def solution(mesh):
    return jax.shard_map(
        body,
        mesh=mesh,
        in_specs=(P(("batch", "blk"), None), P(), P(), P(), P(), P()),
        out_specs=P(("batch", "blk"), None),
        check_vma=False,
    )
```

```python
import functools

import jax
import jax.numpy as jnp
from jax import lax
from jax.experimental import pallas as pl
from jax.experimental.pallas import tpu as pltpu
from jax.sharding import PartitionSpec as P


DILATION_START = 512
EPSILON = 1e-05
CORES = 2
CHUNKS = 2
TILE = 512


VMEM = pl.BlockSpec(memory_space=pltpu.VMEM)
LIMIT = pltpu.CompilerParams(vmem_limit_bytes=12 << 20)


def gelu(x):
    return 0.5 * x * (1.0 + lax.erf(x * (0.5**0.5)))


def project(x, gain, bias, proj):
    values = x.astype(jnp.float32)
    average = jnp.mean(values, axis=1, keepdims=True)
    centred = values - average
    variance = jnp.mean(centred * centred, axis=1, keepdims=True)
    normed = (centred * lax.rsqrt(variance + EPSILON) * gain + bias).astype(jnp.bfloat16)
    return jnp.dot(normed, proj, preferred_element_type=jnp.float32).astype(jnp.bfloat16)


def advance(x, earlier, middle, after, taps, output):
    convolved = jnp.dot(middle, taps[1], preferred_element_type=jnp.float32)
    convolved = convolved + jnp.dot(earlier, taps[0], preferred_element_type=jnp.float32)
    convolved = convolved + jnp.dot(after, taps[2], preferred_element_type=jnp.float32)
    activated = gelu(convolved).astype(jnp.bfloat16)
    update = jnp.dot(activated, output, preferred_element_type=jnp.float32)
    return (x.astype(jnp.float32) + update).astype(jnp.bfloat16)


def tiles(rows):
    size = min(TILE, rows)
    return [slice(r, r + size) for r in range(0, rows, size)]


def position():
    index = lax.axis_index("blk")
    return index // CORES, index % CORES


def enter_kernel(chips, width, *refs):
    pieces, (gain, bias, proj, x_ref, narrow_ref) = refs[:chips], refs[chips:]
    chip, _ = position()
    for k in range(chips):
        x_ref[pl.ds(pl.multiple_of((chip ^ k) * width, width), width), :] = pieces[k][...]
    for t in tiles(chips * width):
        narrow_ref[t, :] = project(x_ref[t, :], gain[0:1, :], bias[0:1, :], proj[0])


def load_partner(partner, padded, chips, width):
    rows = chips * width
    padded[pl.ds(width, rows), :] = partner[...]
    padded[pl.ds(0, width), :] = partner[pl.ds(rows - width, width), :]
    padded[pl.ds(width + rows, width), :] = partner[pl.ds(0, width), :]


def slot_kernel(chips, width, slots, block, x_in, narrow, partner, gain, bias, taps, output, proj,
                x_ref, narrow_ref, padded, earlier, after):
    _, core = position()
    load_partner(partner, padded, chips, width)
    part = width // slots
    shift = 2**block
    for c in range(chips):
        for slot in range(slots):
            to = pl.ds(c * width + slot * part, part)
            if slot >= shift:
                earlier[to, :] = narrow[pl.ds(c * width + (slot - shift) * part, part), :]
            else:
                at = (c + core) * width + (slot - shift + slots) * part
                earlier[to, :] = padded[pl.ds(pl.multiple_of(at, part), part), :]
            if slot + shift < slots:
                after[to, :] = narrow[pl.ds(c * width + (slot + shift) * part, part), :]
            else:
                at = (c + core + 1) * width + (slot + shift - slots) * part
                after[to, :] = padded[pl.ds(pl.multiple_of(at, part), part), :]
    for t in tiles(chips * width):
        x = advance(x_in[t, :], earlier[t, :], narrow[t, :], after[t, :], taps.at[block], output[block])
        x_ref[t, :] = x
        narrow_ref[t, :] = project(
            x, gain[block + 1 : block + 2, :], bias[block + 1 : block + 2, :], proj[block + 1]
        )


def rest_kernel(chips, width, first, layers, x_in, narrow, partner, gain, bias, taps, output, proj, *refs):
    pieces, (padded, own, x_ref) = refs[:chips], refs[chips:]
    blocks = range(first, layers)
    rows = chips * width
    chip, core = position()
    load_partner(partner, padded, chips, width)
    pad = (own.shape[1] - rows) // 2
    for n, block in enumerate(blocks):
        for t in tiles(rows):
            size = t.stop - t.start
            if n == 0:
                x = x_in[t, :]
                middle = narrow[t, :]
                earlier = padded[pl.ds(pl.multiple_of(core * width + t.start, width), size), :]
                after = padded[pl.ds(pl.multiple_of((core + 1) * width + t.start, width), size), :]
            else:
                x = x_ref[t, :]
                shift = 2 ** (n - 1) * width
                held = own.at[n - 1]
                middle = held[pl.ds(pad + t.start, size), :]
                earlier = held[pl.ds(pad + t.start - shift, size), :]
                after = held[pl.ds(pad + t.start + shift, size), :]
            x = advance(x, earlier, middle, after, taps.at[block], output[block])
            x_ref[t, :] = x
            if block + 1 < layers:
                own[n, pl.ds(pad + t.start, size), :] = project(
                    x, gain[block + 1 : block + 2, :], bias[block + 1 : block + 2, :], proj[block + 1]
                )
        if block + 1 < layers:
            own[n, pl.ds(0, pad), :] = own[n, pl.ds(rows, pad), :]
            own[n, pl.ds(pad + rows, pad), :] = own[n, pl.ds(pad, pad), :]
    for k in range(chips):
        pieces[k][...] = x_ref[pl.ds(pl.multiple_of((chip ^ k) * width, width), width), :]


def estimate(rows, model, neck, blocks):
    return pl.CostEstimate(
        flops=2 * rows * blocks * (2 * model * neck + 3 * neck * neck),
        bytes_accessed=blocks * 2 * (2 * model * neck + 3 * neck * neck) + 8 * rows * model,
        transcendentals=0,
    )


def travel_order(chips):
    half = chips // 2
    far = sorted(range(max(2, half), chips), key=lambda k: (-(k >> 1), k))
    return [*range(2, half), *far, *range(1, min(2, chips))]


def chunk_count(chips):
    return max(1, min(CHUNKS, DILATION_START // chips // 16))


def body(stream, norm_gain, norm_bias, proj_in, convolution_taps, output_projection):
    rows, model = stream.shape
    layers, neck = norm_gain.shape[0], proj_in.shape[2]
    peers = lax.axis_size("blk")
    chips = peers // CORES
    slots = rows // DILATION_START
    span = DILATION_START // chips
    chunks = chunk_count(chips)
    part = span // chunks
    width = slots * part
    count = chips * width
    bf16 = jnp.bfloat16
    chip = lax.axis_index("blk") // CORES

    def to_chip(piece, k):
        return lax.ppermute(piece, "blk", [(i, i ^ (k * CORES)) for i in range(peers)])

    def other_core(narrow):
        return lax.ppermute(narrow, "blk", [(i, i ^ 1) for i in range(peers)])

    shape = jax.ShapeDtypeStruct
    enter = pl.pallas_call(
        functools.partial(enter_kernel, chips, width),
        out_shape=(shape((count, model), bf16), shape((count, neck), bf16)),
        in_specs=[VMEM] * (chips + 3),
        out_specs=(VMEM, VMEM),
        cost_estimate=estimate(count, model, neck, 1),
        compiler_params=LIMIT,
        name="enter",
    )
    slot_block = pl.pallas_call(
        functools.partial(slot_kernel, chips, width, slots, 0),
        out_shape=(shape((count, model), bf16), shape((count, neck), bf16)),
        in_specs=[VMEM] * 8,
        out_specs=(VMEM, VMEM),
        scratch_shapes=[
            pltpu.VMEM((count + 2 * width, neck), bf16),
            pltpu.VMEM((count, neck), bf16),
            pltpu.VMEM((count, neck), bf16),
        ],
        cost_estimate=estimate(count, model, neck, 1),
        compiler_params=LIMIT,
        name="slot_block",
    )
    held = layers - 1
    pad = 2 ** (held - 2) * width
    rest = pl.pallas_call(
        functools.partial(rest_kernel, chips, width, 1, layers),
        out_shape=tuple(shape((width, model), bf16) for _ in range(chips)),
        in_specs=[VMEM] * 8,
        out_specs=tuple(VMEM for _ in range(chips)),
        scratch_shapes=[
            pltpu.VMEM((count + 2 * width, neck), bf16),
            pltpu.VMEM((held - 1, count + 2 * pad, neck), bf16),
            pltpu.VMEM((count, model), bf16),
        ],
        cost_estimate=estimate(count, model, neck, held),
        compiler_params=LIMIT,
        name="rest",
    )

    grid = stream.reshape(slots, chips * chunks, part, model)
    arrived = []
    for j in range(chunks):
        pieces = {}
        for k in [0, *travel_order(chips)]:
            piece = lax.dynamic_slice_in_dim(grid, (chip ^ k) * chunks + j, 1, axis=1).reshape(width, model)
            pieces[k] = to_chip(piece, k) if k else piece
        arrived.append([pieces[k] for k in range(chips)])

    left = []
    for j in range(chunks):
        x, narrow = enter(*arrived[j], norm_gain, norm_bias, proj_in)
        weights = (norm_gain, norm_bias, convolution_taps, output_projection, proj_in)
        x, narrow = slot_block(x, narrow, other_core(narrow), *weights)
        partner = other_core(narrow)
        pieces = rest(x, narrow, partner, *weights)
        gone = {0: pieces[0]}
        for k in travel_order(chips):
            gone[k] = to_chip(pieces[k], k)
        left.append(gone)

    result = jnp.zeros(grid.shape, bf16)
    for j in range(chunks):
        for k in [0, *travel_order(chips)]:
            piece = left[j][k].reshape(slots, 1, part, model)
            result = lax.dynamic_update_slice_in_dim(result, piece, (chip ^ k) * chunks + j, axis=1)
    return result.reshape(rows, model)


def solution(mesh):
    return jax.shard_map(
        body,
        mesh=mesh,
        in_specs=(P(("batch", "blk"), None), P(), P(), P(), P(), P()),
        out_specs=P(("batch", "blk"), None),
        check_vma=False,
    )
```

```python
import functools

import jax
import jax.numpy as jnp
from jax import lax
from jax.experimental import pallas as pl
from jax.experimental.pallas import tpu as pltpu
from jax.sharding import PartitionSpec as P


DILATION_START = 512
EPSILON = 1e-05
CORES = 2
CHUNKS = 2
TILE = 512


VMEM = pl.BlockSpec(memory_space=pltpu.VMEM)
LIMIT = pltpu.CompilerParams(vmem_limit_bytes=12 << 20)


def gelu(x):
    return 0.5 * x * (1.0 + lax.erf(x * (0.5**0.5)))


def project(x, gain, bias, proj):
    values = x.astype(jnp.float32)
    average = jnp.mean(values, axis=1, keepdims=True)
    centred = values - average
    variance = jnp.mean(centred * centred, axis=1, keepdims=True)
    normed = (centred * lax.rsqrt(variance + EPSILON) * gain + bias).astype(jnp.bfloat16)
    return jnp.dot(normed, proj, preferred_element_type=jnp.float32).astype(jnp.bfloat16)


def advance(x, earlier, middle, after, taps, output):
    convolved = jnp.dot(middle, taps[1], preferred_element_type=jnp.float32)
    convolved = convolved + jnp.dot(earlier, taps[0], preferred_element_type=jnp.float32)
    convolved = convolved + jnp.dot(after, taps[2], preferred_element_type=jnp.float32)
    activated = gelu(convolved).astype(jnp.bfloat16)
    update = jnp.dot(activated, output, preferred_element_type=jnp.float32)
    return (x.astype(jnp.float32) + update).astype(jnp.bfloat16)


def tiles(rows):
    size = min(TILE, rows)
    return [slice(r, r + size) for r in range(0, rows, size)]


def position():
    index = lax.axis_index("blk")
    return index // CORES, index % CORES


def load_kernel(taps, output, proj, token):
    token[...] = jnp.zeros_like(token)


def enter_kernel(chips, width, *refs):
    pieces, (gain, bias, proj, _, x_ref, narrow_ref) = refs[:chips], refs[chips:]
    chip, _ = position()
    for k in range(chips):
        x_ref[pl.ds(pl.multiple_of((chip ^ k) * width, width), width), :] = pieces[k][...]
    for t in tiles(chips * width):
        narrow_ref[t, :] = project(x_ref[t, :], gain[0:1, :], bias[0:1, :], proj[0])


def load_partner(partner, padded, chips, width):
    rows = chips * width
    padded[pl.ds(width, rows), :] = partner[...]
    padded[pl.ds(0, width), :] = partner[pl.ds(rows - width, width), :]
    padded[pl.ds(width + rows, width), :] = partner[pl.ds(0, width), :]


def slot_kernel(chips, width, slots, block, x_in, narrow, partner, gain, bias, taps, output, proj,
                x_ref, narrow_ref, padded, earlier, after):
    _, core = position()
    load_partner(partner, padded, chips, width)
    part = width // slots
    shift = 2**block
    for c in range(chips):
        for slot in range(slots):
            to = pl.ds(c * width + slot * part, part)
            if slot >= shift:
                earlier[to, :] = narrow[pl.ds(c * width + (slot - shift) * part, part), :]
            else:
                at = (c + core) * width + (slot - shift + slots) * part
                earlier[to, :] = padded[pl.ds(pl.multiple_of(at, part), part), :]
            if slot + shift < slots:
                after[to, :] = narrow[pl.ds(c * width + (slot + shift) * part, part), :]
            else:
                at = (c + core + 1) * width + (slot + shift - slots) * part
                after[to, :] = padded[pl.ds(pl.multiple_of(at, part), part), :]
    for t in tiles(chips * width):
        x = advance(x_in[t, :], earlier[t, :], narrow[t, :], after[t, :], taps.at[block], output[block])
        x_ref[t, :] = x
        narrow_ref[t, :] = project(
            x, gain[block + 1 : block + 2, :], bias[block + 1 : block + 2, :], proj[block + 1]
        )


def rest_kernel(chips, width, first, layers, x_in, narrow, partner, gain, bias, taps, output, proj, *refs):
    pieces, (padded, own, x_ref) = refs[:chips], refs[chips:]
    blocks = range(first, layers)
    rows = chips * width
    chip, core = position()
    load_partner(partner, padded, chips, width)
    pad = (own.shape[1] - rows) // 2
    for n, block in enumerate(blocks):
        for t in tiles(rows):
            size = t.stop - t.start
            if n == 0:
                x = x_in[t, :]
                middle = narrow[t, :]
                earlier = padded[pl.ds(pl.multiple_of(core * width + t.start, width), size), :]
                after = padded[pl.ds(pl.multiple_of((core + 1) * width + t.start, width), size), :]
            else:
                x = x_ref[t, :]
                shift = 2 ** (n - 1) * width
                held = own.at[n - 1]
                middle = held[pl.ds(pad + t.start, size), :]
                earlier = held[pl.ds(pad + t.start - shift, size), :]
                after = held[pl.ds(pad + t.start + shift, size), :]
            x = advance(x, earlier, middle, after, taps.at[block], output[block])
            x_ref[t, :] = x
            if block + 1 < layers:
                own[n, pl.ds(pad + t.start, size), :] = project(
                    x, gain[block + 1 : block + 2, :], bias[block + 1 : block + 2, :], proj[block + 1]
                )
        if block + 1 < layers:
            own[n, pl.ds(0, pad), :] = own[n, pl.ds(rows, pad), :]
            own[n, pl.ds(pad + rows, pad), :] = own[n, pl.ds(pad, pad), :]
    for k in range(chips):
        pieces[k][...] = x_ref[pl.ds(pl.multiple_of((chip ^ k) * width, width), width), :]


def estimate(rows, model, neck, blocks):
    return pl.CostEstimate(
        flops=2 * rows * blocks * (2 * model * neck + 3 * neck * neck),
        bytes_accessed=blocks * 2 * (2 * model * neck + 3 * neck * neck) + 8 * rows * model,
        transcendentals=0,
    )


def travel_order(chips):
    half = chips // 2
    far = sorted(range(max(2, half), chips), key=lambda k: (-(k >> 1), k))
    return [*range(2, half), *far, *range(1, min(2, chips))]


def chunk_count(chips):
    return max(1, min(CHUNKS, DILATION_START // chips // 16))


def body(stream, norm_gain, norm_bias, proj_in, convolution_taps, output_projection):
    rows, model = stream.shape
    layers, neck = norm_gain.shape[0], proj_in.shape[2]
    peers = lax.axis_size("blk")
    chips = peers // CORES
    slots = rows // DILATION_START
    span = DILATION_START // chips
    chunks = chunk_count(chips)
    part = span // chunks
    width = slots * part
    count = chips * width
    bf16 = jnp.bfloat16
    chip = lax.axis_index("blk") // CORES

    def to_chip(piece, k):
        return lax.ppermute(piece, "blk", [(i, i ^ (k * CORES)) for i in range(peers)])

    def other_core(narrow):
        return lax.ppermute(narrow, "blk", [(i, i ^ 1) for i in range(peers)])

    shape = jax.ShapeDtypeStruct
    load = pl.pallas_call(
        load_kernel,
        out_shape=shape((8, 128), jnp.float32),
        in_specs=[VMEM] * 3,
        out_specs=VMEM,
        compiler_params=LIMIT,
        name="load",
    )
    enter = pl.pallas_call(
        functools.partial(enter_kernel, chips, width),
        out_shape=(shape((count, model), bf16), shape((count, neck), bf16)),
        in_specs=[VMEM] * (chips + 4),
        out_specs=(VMEM, VMEM),
        cost_estimate=estimate(count, model, neck, 1),
        compiler_params=LIMIT,
        name="enter",
    )
    slot_block = pl.pallas_call(
        functools.partial(slot_kernel, chips, width, slots, 0),
        out_shape=(shape((count, model), bf16), shape((count, neck), bf16)),
        in_specs=[VMEM] * 8,
        out_specs=(VMEM, VMEM),
        scratch_shapes=[
            pltpu.VMEM((count + 2 * width, neck), bf16),
            pltpu.VMEM((count, neck), bf16),
            pltpu.VMEM((count, neck), bf16),
        ],
        cost_estimate=estimate(count, model, neck, 1),
        compiler_params=LIMIT,
        name="slot_block",
    )
    held = layers - 1
    pad = 2 ** (held - 2) * width
    rest = pl.pallas_call(
        functools.partial(rest_kernel, chips, width, 1, layers),
        out_shape=tuple(shape((width, model), bf16) for _ in range(chips)),
        in_specs=[VMEM] * 8,
        out_specs=tuple(VMEM for _ in range(chips)),
        scratch_shapes=[
            pltpu.VMEM((count + 2 * width, neck), bf16),
            pltpu.VMEM((held - 1, count + 2 * pad, neck), bf16),
            pltpu.VMEM((count, model), bf16),
        ],
        cost_estimate=estimate(count, model, neck, held),
        compiler_params=LIMIT,
        name="rest",
    )

    grid = stream.reshape(slots, chips * chunks, part, model)
    arrived = []
    for j in range(chunks):
        pieces = {}
        for k in [0, *travel_order(chips)]:
            piece = lax.dynamic_slice_in_dim(grid, (chip ^ k) * chunks + j, 1, axis=1).reshape(width, model)
            pieces[k] = to_chip(piece, k) if k else piece
        arrived.append([pieces[k] for k in range(chips)])

    weights = (norm_gain, norm_bias, convolution_taps, output_projection, proj_in)
    token = load(convolution_taps, output_projection, proj_in)
    left = []
    for j in range(chunks):
        x, narrow = enter(*arrived[j], norm_gain, norm_bias, proj_in, token)
        partner = other_core(narrow)
        x, narrow = slot_block(x, narrow, partner, *weights)
        partner = other_core(narrow)
        pieces = rest(x, narrow, partner, *weights)
        gone = {0: pieces[0]}
        for k in travel_order(chips):
            gone[k] = to_chip(pieces[k], k)
        left.append(gone)

    result = jnp.zeros(grid.shape, bf16)
    for j in range(chunks):
        for k in [0, *travel_order(chips)]:
            piece = left[j][k].reshape(slots, 1, part, model)
            result = lax.dynamic_update_slice_in_dim(result, piece, (chip ^ k) * chunks + j, axis=1)
    return result.reshape(rows, model)


def solution(mesh):
    return jax.shard_map(
        body,
        mesh=mesh,
        in_specs=(P(("batch", "blk"), None), P(), P(), P(), P(), P()),
        out_specs=P(("batch", "blk"), None),
        check_vma=False,
    )
```

```python
import functools

import jax
import jax.numpy as jnp
from jax import lax
from jax.experimental import pallas as pl
from jax.experimental.pallas import tpu as pltpu
from jax.sharding import PartitionSpec as P


DILATION_START = 512
EPSILON = 1e-05
CORES = 2
CHUNKS = 2
TILE = 512


VMEM = pl.BlockSpec(memory_space=pltpu.VMEM)
LIMIT = pltpu.CompilerParams(vmem_limit_bytes=12 << 20)


def gelu(x):
    return 0.5 * x * (1.0 + lax.erf(x * (0.5**0.5)))


def project(x, gain, bias, proj):
    values = x.astype(jnp.float32)
    average = jnp.mean(values, axis=1, keepdims=True)
    centred = values - average
    variance = jnp.mean(centred * centred, axis=1, keepdims=True)
    normed = (centred * lax.rsqrt(variance + EPSILON) * gain + bias).astype(jnp.bfloat16)
    return jnp.dot(normed, proj, preferred_element_type=jnp.float32).astype(jnp.bfloat16)


def advance(x, earlier, middle, after, taps, output):
    convolved = jnp.dot(middle, taps[1], preferred_element_type=jnp.float32)
    convolved = convolved + jnp.dot(earlier, taps[0], preferred_element_type=jnp.float32)
    convolved = convolved + jnp.dot(after, taps[2], preferred_element_type=jnp.float32)
    activated = gelu(convolved).astype(jnp.bfloat16)
    update = jnp.dot(activated, output, preferred_element_type=jnp.float32)
    return (x.astype(jnp.float32) + update).astype(jnp.bfloat16)


def tiles(rows):
    size = min(TILE, rows)
    return [slice(r, r + size) for r in range(0, rows, size)]


def position():
    index = lax.axis_index("blk")
    return index // CORES, index % CORES


def load_kernel(taps, output, proj, token):
    token[...] = jnp.zeros_like(token)


def enter_kernel(chips, width, *refs):
    pieces, (gain, bias, proj, _, x_ref, narrow_ref) = refs[:chips], refs[chips:]
    chip, _ = position()
    for k in range(chips):
        x_ref[pl.ds(pl.multiple_of((chip ^ k) * width, width), width), :] = pieces[k][...]
    for t in tiles(chips * width):
        narrow_ref[t, :] = project(x_ref[t, :], gain[0:1, :], bias[0:1, :], proj[0])


def load_partner(partner, padded, chips, width):
    rows = chips * width
    padded[pl.ds(width, rows), :] = partner[...]
    padded[pl.ds(0, width), :] = partner[pl.ds(rows - width, width), :]
    padded[pl.ds(width + rows, width), :] = partner[pl.ds(0, width), :]


def slot_kernel(chips, width, slots, block, x_in, narrow, partner, gain, bias, taps, output, proj,
                x_ref, narrow_ref, padded, earlier, after):
    _, core = position()
    load_partner(partner, padded, chips, width)
    part = width // slots
    shift = 2**block
    for c in range(chips):
        for slot in range(slots):
            to = pl.ds(c * width + slot * part, part)
            if slot >= shift:
                earlier[to, :] = narrow[pl.ds(c * width + (slot - shift) * part, part), :]
            else:
                at = (c + core) * width + (slot - shift + slots) * part
                earlier[to, :] = padded[pl.ds(pl.multiple_of(at, part), part), :]
            if slot + shift < slots:
                after[to, :] = narrow[pl.ds(c * width + (slot + shift) * part, part), :]
            else:
                at = (c + core + 1) * width + (slot + shift - slots) * part
                after[to, :] = padded[pl.ds(pl.multiple_of(at, part), part), :]
    for t in tiles(chips * width):
        x = advance(x_in[t, :], earlier[t, :], narrow[t, :], after[t, :], taps.at[block], output[block])
        x_ref[t, :] = x
        narrow_ref[t, :] = project(
            x, gain[block + 1 : block + 2, :], bias[block + 1 : block + 2, :], proj[block + 1]
        )


def rest_kernel(chips, width, first, layers, x_in, narrow, partner, gain, bias, taps, output, proj, *refs):
    pieces, (padded, own, x_ref) = refs[:chips], refs[chips:]
    blocks = range(first, layers)
    rows = chips * width
    chip, core = position()
    load_partner(partner, padded, chips, width)
    pad = (own.shape[1] - rows) // 2
    for n, block in enumerate(blocks):
        for t in tiles(rows):
            size = t.stop - t.start
            if n == 0:
                x = x_in[t, :]
                middle = narrow[t, :]
                earlier = padded[pl.ds(pl.multiple_of(core * width + t.start, width), size), :]
                after = padded[pl.ds(pl.multiple_of((core + 1) * width + t.start, width), size), :]
            else:
                x = x_ref[t, :]
                shift = 2 ** (n - 1) * width
                held = own.at[n - 1]
                middle = held[pl.ds(pad + t.start, size), :]
                earlier = held[pl.ds(pad + t.start - shift, size), :]
                after = held[pl.ds(pad + t.start + shift, size), :]
            x = advance(x, earlier, middle, after, taps.at[block], output[block])
            x_ref[t, :] = x
            if block + 1 < layers:
                own[n, pl.ds(pad + t.start, size), :] = project(
                    x, gain[block + 1 : block + 2, :], bias[block + 1 : block + 2, :], proj[block + 1]
                )
        if block + 1 < layers:
            own[n, pl.ds(0, pad), :] = own[n, pl.ds(rows, pad), :]
            own[n, pl.ds(pad + rows, pad), :] = own[n, pl.ds(pad, pad), :]
    for k in range(chips):
        pieces[k][...] = x_ref[pl.ds(pl.multiple_of((chip ^ k) * width, width), width), :]


def collect_kernel(chips, slots, part, chunks, chunk, *refs):
    pieces, (result, sems) = refs[:chips], refs[-2:]
    chip, _ = position()
    copies = [
        pltpu.make_async_copy(
            pieces[k].at[pl.ds(slot * part, part), :],
            result.at[slot, (chip ^ k) * chunks + chunk],
            sems.at[k, slot],
        )
        for k in range(chips)
        for slot in range(slots)
    ]
    for copy in copies:
        copy.start()
    for copy in copies:
        copy.wait()


def estimate(rows, model, neck, blocks):
    return pl.CostEstimate(
        flops=2 * rows * blocks * (2 * model * neck + 3 * neck * neck),
        bytes_accessed=blocks * 2 * (2 * model * neck + 3 * neck * neck) + 8 * rows * model,
        transcendentals=0,
    )


def travel_order(chips):
    half = chips // 2
    far = sorted(range(max(2, half), chips), key=lambda k: (-(k >> 1), k))
    return list(range(2, half)), far, list(range(1, min(2, chips)))


def leave_order(chips):
    near, far, next_to = travel_order(chips)
    return far[:2] + near + far[2:] + next_to


def chunk_count(chips):
    return max(1, min(CHUNKS, DILATION_START // chips // 16))


def body(stream, norm_gain, norm_bias, proj_in, convolution_taps, output_projection):
    rows, model = stream.shape
    layers, neck = norm_gain.shape[0], proj_in.shape[2]
    peers = lax.axis_size("blk")
    chips = peers // CORES
    slots = rows // DILATION_START
    span = DILATION_START // chips
    chunks = chunk_count(chips)
    part = span // chunks
    width = slots * part
    count = chips * width
    bf16 = jnp.bfloat16
    chip = lax.axis_index("blk") // CORES

    def to_chip(piece, k):
        return lax.ppermute(piece, "blk", [(i, i ^ (k * CORES)) for i in range(peers)])

    def other_core(narrow):
        return lax.ppermute(narrow, "blk", [(i, i ^ 1) for i in range(peers)])

    shape = jax.ShapeDtypeStruct
    load = pl.pallas_call(
        load_kernel,
        out_shape=shape((8, 128), jnp.float32),
        in_specs=[VMEM] * 3,
        out_specs=VMEM,
        compiler_params=LIMIT,
        name="load",
    )
    enter = pl.pallas_call(
        functools.partial(enter_kernel, chips, width),
        out_shape=(shape((count, model), bf16), shape((count, neck), bf16)),
        in_specs=[VMEM] * (chips + 4),
        out_specs=(VMEM, VMEM),
        cost_estimate=estimate(count, model, neck, 1),
        compiler_params=LIMIT,
        name="enter",
    )
    slot_block = pl.pallas_call(
        functools.partial(slot_kernel, chips, width, slots, 0),
        out_shape=(shape((count, model), bf16), shape((count, neck), bf16)),
        in_specs=[VMEM] * 8,
        out_specs=(VMEM, VMEM),
        scratch_shapes=[
            pltpu.VMEM((count + 2 * width, neck), bf16),
            pltpu.VMEM((count, neck), bf16),
            pltpu.VMEM((count, neck), bf16),
        ],
        cost_estimate=estimate(count, model, neck, 1),
        compiler_params=LIMIT,
        name="slot_block",
    )
    held = layers - 1
    pad = 2 ** (held - 2) * width
    rest = pl.pallas_call(
        functools.partial(rest_kernel, chips, width, 1, layers),
        out_shape=tuple(shape((width, model), bf16) for _ in range(chips)),
        in_specs=[VMEM] * 8,
        out_specs=tuple(VMEM for _ in range(chips)),
        scratch_shapes=[
            pltpu.VMEM((count + 2 * width, neck), bf16),
            pltpu.VMEM((held - 1, count + 2 * pad, neck), bf16),
            pltpu.VMEM((count, model), bf16),
        ],
        cost_estimate=estimate(count, model, neck, held),
        compiler_params=LIMIT,
        name="rest",
    )

    grid = stream.reshape(slots, chips * chunks, part, model)
    arrived = []
    for j in range(chunks):
        pieces = {}
        grid = lax.optimization_barrier(grid)
        for k in [0, *leave_order(chips)]:
            piece = lax.dynamic_slice_in_dim(grid, (chip ^ k) * chunks + j, 1, axis=1).reshape(width, model)
            pieces[k] = to_chip(piece, k) if k else piece
        arrived.append([pieces[k] for k in range(chips)])

    weights = (norm_gain, norm_bias, convolution_taps, output_projection, proj_in)
    token = load(convolution_taps, output_projection, proj_in)
    left = []
    for j in range(chunks):
        x, narrow = enter(*arrived[j], norm_gain, norm_bias, proj_in, token)
        partner = other_core(narrow)
        x, narrow = slot_block(x, narrow, partner, *weights)
        partner = other_core(narrow)
        pieces = rest(x, narrow, partner, *weights)
        gone = {0: pieces[0]}
        for k in leave_order(chips):
            gone[k] = to_chip(pieces[k], k)
        left.append(gone)

    result = None
    for j in range(chunks):
        collect = pl.pallas_call(
            functools.partial(collect_kernel, chips, slots, part, chunks, j),
            out_shape=shape(grid.shape, bf16),
            in_specs=[VMEM] * chips + [pl.BlockSpec(memory_space=pl.ANY)] * (j > 0),
            out_specs=pl.BlockSpec(memory_space=pl.ANY),
            scratch_shapes=[pltpu.SemaphoreType.DMA((chips, slots))],
            input_output_aliases={chips: 0} if j else {},
            compiler_params=LIMIT,
            name="collect",
        )
        result = collect(*[left[j][k] for k in range(chips)], *([result] if j else []))
    return result.reshape(rows, model)


def solution(mesh):
    return jax.shard_map(
        body,
        mesh=mesh,
        in_specs=(P(("batch", "blk"), None), P(), P(), P(), P(), P()),
        out_specs=P(("batch", "blk"), None),
        check_vma=False,
    )
```

```python
import functools

import jax
import jax.numpy as jnp
from jax import lax
from jax.experimental import pallas as pl
from jax.experimental.pallas import tpu as pltpu
from jax.sharding import PartitionSpec as P


DILATION_START = 512
EPSILON = 1e-05
CORES = 2
CHUNKS = 2
TILE = 512


VMEM = pl.BlockSpec(memory_space=pltpu.VMEM)
LIMIT = pltpu.CompilerParams(vmem_limit_bytes=12 << 20)


def gelu(x):
    return 0.5 * x * (1.0 + lax.erf(x * (0.5**0.5)))


def project(x, gain, bias, proj):
    values = x.astype(jnp.float32)
    average = jnp.mean(values, axis=1, keepdims=True)
    centred = values - average
    variance = jnp.mean(centred * centred, axis=1, keepdims=True)
    normed = (centred * lax.rsqrt(variance + EPSILON) * gain + bias).astype(jnp.bfloat16)
    return jnp.dot(normed, proj, preferred_element_type=jnp.float32).astype(jnp.bfloat16)


def advance(x, earlier, middle, after, taps, output):
    convolved = jnp.dot(middle, taps[1], preferred_element_type=jnp.float32)
    convolved = convolved + jnp.dot(earlier, taps[0], preferred_element_type=jnp.float32)
    convolved = convolved + jnp.dot(after, taps[2], preferred_element_type=jnp.float32)
    activated = gelu(convolved).astype(jnp.bfloat16)
    update = jnp.dot(activated, output, preferred_element_type=jnp.float32)
    return (x.astype(jnp.float32) + update).astype(jnp.bfloat16)


def tiles(rows):
    size = min(TILE, rows)
    return [slice(r, r + size) for r in range(0, rows, size)]


def position():
    index = lax.axis_index("blk")
    return index // CORES, index % CORES


def load_kernel(taps, output, proj, token):
    token[...] = jnp.zeros_like(token)


def enter_kernel(chips, width, *refs):
    pieces, (gain, bias, proj, _, x_ref, narrow_ref) = refs[:chips], refs[chips:]
    chip, _ = position()
    for k in range(chips):
        x_ref[pl.ds(pl.multiple_of((chip ^ k) * width, width), width), :] = pieces[k][...]
    for t in tiles(chips * width):
        narrow_ref[t, :] = project(x_ref[t, :], gain[0:1, :], bias[0:1, :], proj[0])


def load_partner(partner, padded, chips, width):
    rows = chips * width
    padded[pl.ds(width, rows), :] = partner[...]
    padded[pl.ds(0, width), :] = partner[pl.ds(rows - width, width), :]
    padded[pl.ds(width + rows, width), :] = partner[pl.ds(0, width), :]


def slot_kernel(chips, width, slots, block, x_in, narrow, partner, gain, bias, taps, output, proj,
                x_ref, narrow_ref, padded, earlier, after):
    _, core = position()
    load_partner(partner, padded, chips, width)
    part = width // slots
    shift = 2**block
    for c in range(chips):
        for slot in range(slots):
            to = pl.ds(c * width + slot * part, part)
            if slot >= shift:
                earlier[to, :] = narrow[pl.ds(c * width + (slot - shift) * part, part), :]
            else:
                at = (c + core) * width + (slot - shift + slots) * part
                earlier[to, :] = padded[pl.ds(pl.multiple_of(at, part), part), :]
            if slot + shift < slots:
                after[to, :] = narrow[pl.ds(c * width + (slot + shift) * part, part), :]
            else:
                at = (c + core + 1) * width + (slot + shift - slots) * part
                after[to, :] = padded[pl.ds(pl.multiple_of(at, part), part), :]
    for t in tiles(chips * width):
        x = advance(x_in[t, :], earlier[t, :], narrow[t, :], after[t, :], taps.at[block], output[block])
        x_ref[t, :] = x
        narrow_ref[t, :] = project(
            x, gain[block + 1 : block + 2, :], bias[block + 1 : block + 2, :], proj[block + 1]
        )


def rest_kernel(chips, width, first, layers, x_in, narrow, partner, gain, bias, taps, output, proj, *refs):
    pieces, (padded, own, x_ref) = refs[:chips], refs[chips:]
    blocks = range(first, layers)
    rows = chips * width
    chip, core = position()
    load_partner(partner, padded, chips, width)
    pad = (own.shape[1] - rows) // 2
    for n, block in enumerate(blocks):
        for t in tiles(rows):
            size = t.stop - t.start
            if n == 0:
                x = x_in[t, :]
                middle = narrow[t, :]
                earlier = padded[pl.ds(pl.multiple_of(core * width + t.start, width), size), :]
                after = padded[pl.ds(pl.multiple_of((core + 1) * width + t.start, width), size), :]
            else:
                x = x_ref[t, :]
                shift = 2 ** (n - 1) * width
                held = own.at[n - 1]
                middle = held[pl.ds(pad + t.start, size), :]
                earlier = held[pl.ds(pad + t.start - shift, size), :]
                after = held[pl.ds(pad + t.start + shift, size), :]
            x = advance(x, earlier, middle, after, taps.at[block], output[block])
            x_ref[t, :] = x
            if block + 1 < layers:
                own[n, pl.ds(pad + t.start, size), :] = project(
                    x, gain[block + 1 : block + 2, :], bias[block + 1 : block + 2, :], proj[block + 1]
                )
        if block + 1 < layers:
            own[n, pl.ds(0, pad), :] = own[n, pl.ds(rows, pad), :]
            own[n, pl.ds(pad + rows, pad), :] = own[n, pl.ds(pad, pad), :]
    for k in range(chips):
        pieces[k][...] = x_ref[pl.ds(pl.multiple_of((chip ^ k) * width, width), width), :]


def collect_kernel(ways, slots, part, chunks, chunk, *refs):
    pieces, (result, sems) = refs[: len(ways)], refs[-2:]
    chip, _ = position()
    copies = [
        pltpu.make_async_copy(
            pieces[n].at[pl.ds(slot * part, part), :],
            result.at[slot, (chip ^ k) * chunks + chunk],
            sems.at[n, slot],
        )
        for n, k in enumerate(ways)
        for slot in range(slots)
    ]
    for copy in copies:
        copy.start()
    for copy in copies:
        copy.wait()


def estimate(rows, model, neck, blocks):
    return pl.CostEstimate(
        flops=2 * rows * blocks * (2 * model * neck + 3 * neck * neck),
        bytes_accessed=blocks * 2 * (2 * model * neck + 3 * neck * neck) + 8 * rows * model,
        transcendentals=0,
    )


def travel_order(chips):
    half = chips // 2
    far = sorted(range(max(2, half), chips), key=lambda k: (-(k >> 1), k))
    return list(range(2, half)), far, list(range(1, min(2, chips)))


def leave_order(chips):
    near, far, next_to = travel_order(chips)
    return far[:2] + near + far[2:] + next_to


def chunk_count(chips):
    return max(1, min(CHUNKS, DILATION_START // chips // 16))


def body(stream, norm_gain, norm_bias, proj_in, convolution_taps, output_projection):
    rows, model = stream.shape
    layers, neck = norm_gain.shape[0], proj_in.shape[2]
    peers = lax.axis_size("blk")
    chips = peers // CORES
    slots = rows // DILATION_START
    span = DILATION_START // chips
    chunks = chunk_count(chips)
    part = span // chunks
    width = slots * part
    count = chips * width
    bf16 = jnp.bfloat16
    chip = lax.axis_index("blk") // CORES

    def to_chip(piece, k):
        return lax.ppermute(piece, "blk", [(i, i ^ (k * CORES)) for i in range(peers)])

    def other_core(narrow):
        return lax.ppermute(narrow, "blk", [(i, i ^ 1) for i in range(peers)])

    shape = jax.ShapeDtypeStruct
    load = pl.pallas_call(
        load_kernel,
        out_shape=shape((8, 128), jnp.float32),
        in_specs=[VMEM] * 3,
        out_specs=VMEM,
        compiler_params=LIMIT,
        name="load",
    )
    enter = pl.pallas_call(
        functools.partial(enter_kernel, chips, width),
        out_shape=(shape((count, model), bf16), shape((count, neck), bf16)),
        in_specs=[VMEM] * (chips + 4),
        out_specs=(VMEM, VMEM),
        cost_estimate=estimate(count, model, neck, 1),
        compiler_params=LIMIT,
        name="enter",
    )
    slot_block = pl.pallas_call(
        functools.partial(slot_kernel, chips, width, slots, 0),
        out_shape=(shape((count, model), bf16), shape((count, neck), bf16)),
        in_specs=[VMEM] * 8,
        out_specs=(VMEM, VMEM),
        scratch_shapes=[
            pltpu.VMEM((count + 2 * width, neck), bf16),
            pltpu.VMEM((count, neck), bf16),
            pltpu.VMEM((count, neck), bf16),
        ],
        cost_estimate=estimate(count, model, neck, 1),
        compiler_params=LIMIT,
        name="slot_block",
    )
    held = layers - 1
    pad = 2 ** (held - 2) * width
    rest = pl.pallas_call(
        functools.partial(rest_kernel, chips, width, 1, layers),
        out_shape=tuple(shape((width, model), bf16) for _ in range(chips)),
        in_specs=[VMEM] * 8,
        out_specs=tuple(VMEM for _ in range(chips)),
        scratch_shapes=[
            pltpu.VMEM((count + 2 * width, neck), bf16),
            pltpu.VMEM((held - 1, count + 2 * pad, neck), bf16),
            pltpu.VMEM((count, model), bf16),
        ],
        cost_estimate=estimate(count, model, neck, held),
        compiler_params=LIMIT,
        name="rest",
    )

    grid = stream.reshape(slots, chips * chunks, part, model)
    arrived = []
    for j in range(chunks):
        pieces = {}
        grid = lax.optimization_barrier(grid)
        for n, k in enumerate([*leave_order(chips), 0]):
            if j == 0 and n == 2:
                grid = lax.optimization_barrier(grid)
            piece = lax.dynamic_slice_in_dim(grid, (chip ^ k) * chunks + j, 1, axis=1).reshape(width, model)
            pieces[k] = to_chip(piece, k) if k else piece
        arrived.append([pieces[k] for k in range(chips)])

    weights = (norm_gain, norm_bias, convolution_taps, output_projection, proj_in)
    token = load(convolution_taps, output_projection, proj_in)
    left = []
    for j in range(chunks):
        x, narrow = enter(*arrived[j], norm_gain, norm_bias, proj_in, token)
        partner = other_core(narrow)
        x, narrow = slot_block(x, narrow, partner, *weights)
        partner = other_core(narrow)
        pieces = rest(x, narrow, partner, *weights)
        gone = {0: pieces[0]}
        for k in leave_order(chips):
            gone[k] = to_chip(pieces[k], k)
        left.append(gone)

    result = None
    leave = [0, *leave_order(chips)]
    late = travel_order(chips)[1][2:]
    groups = [(j, leave) for j in range(chunks - 1)]
    groups += [(chunks - 1, [k for k in leave if k not in late]), (chunks - 1, late)]
    for n, (j, ways) in enumerate(groups):
        collect = pl.pallas_call(
            functools.partial(collect_kernel, ways, slots, part, chunks, j),
            out_shape=shape(grid.shape, bf16),
            in_specs=[VMEM] * len(ways) + [pl.BlockSpec(memory_space=pl.ANY)] * (n > 0),
            out_specs=pl.BlockSpec(memory_space=pl.ANY),
            scratch_shapes=[pltpu.SemaphoreType.DMA((len(ways), slots))],
            input_output_aliases={len(ways): 0} if n else {},
            compiler_params=LIMIT,
            name="collect",
        )
        result = collect(*[left[j][k] for k in ways], *([result] if n else []))
    return result.reshape(rows, model)


def solution(mesh):
    return jax.shard_map(
        body,
        mesh=mesh,
        in_specs=(P(("batch", "blk"), None), P(), P(), P(), P(), P()),
        out_specs=P(("batch", "blk"), None),
        check_vma=False,
    )
```

```python
import functools

import jax
import jax.numpy as jnp
from jax import lax
from jax.experimental import pallas as pl
from jax.experimental.pallas import tpu as pltpu
from jax.sharding import PartitionSpec as P


DILATION_START = 512
EPSILON = 1e-05
CORES = 2
CHUNKS = 2
TILE = 512


VMEM = pl.BlockSpec(memory_space=pltpu.VMEM)
LIMIT = pltpu.CompilerParams(vmem_limit_bytes=12 << 20)


def gelu(x):
    return 0.5 * x * (1.0 + lax.erf(x * (0.5**0.5)))


def project(x, gain, bias, proj):
    values = x.astype(jnp.float32)
    average = jnp.mean(values, axis=1, keepdims=True)
    centred = values - average
    variance = jnp.mean(centred * centred, axis=1, keepdims=True)
    normed = (centred * lax.rsqrt(variance + EPSILON) * gain + bias).astype(jnp.bfloat16)
    return jnp.dot(normed, proj, preferred_element_type=jnp.float32).astype(jnp.bfloat16)


def advance(x, earlier, middle, after, taps, output):
    convolved = jnp.dot(middle, taps[1], preferred_element_type=jnp.float32)
    convolved = convolved + jnp.dot(earlier, taps[0], preferred_element_type=jnp.float32)
    convolved = convolved + jnp.dot(after, taps[2], preferred_element_type=jnp.float32)
    activated = gelu(convolved).astype(jnp.bfloat16)
    update = jnp.dot(activated, output, preferred_element_type=jnp.float32)
    return (x.astype(jnp.float32) + update).astype(jnp.bfloat16)


def tiles(rows):
    size = min(TILE, rows)
    return [slice(r, r + size) for r in range(0, rows, size)]


def position():
    index = lax.axis_index("blk")
    return index // CORES, index % CORES


def load_kernel(taps, output, proj, token):
    token[...] = jnp.zeros_like(token)


def enter_kernel(chips, width, *refs):
    pieces, (gain, bias, proj, _, x_ref, narrow_ref) = refs[:chips], refs[chips:]
    chip, _ = position()
    for k in range(chips):
        x_ref[pl.ds(pl.multiple_of((chip ^ k) * width, width), width), :] = pieces[k][...]
    for t in tiles(chips * width):
        narrow_ref[t, :] = project(x_ref[t, :], gain[0:1, :], bias[0:1, :], proj[0])


def load_partner(partner, padded, chips, width):
    rows = chips * width
    padded[pl.ds(width, rows), :] = partner[...]
    padded[pl.ds(0, width), :] = partner[pl.ds(rows - width, width), :]
    padded[pl.ds(width + rows, width), :] = partner[pl.ds(0, width), :]


def slot_kernel(chips, width, slots, block, x_in, narrow, partner, gain, bias, taps, output, proj,
                x_ref, narrow_ref, padded, earlier, after):
    _, core = position()
    load_partner(partner, padded, chips, width)
    part = width // slots
    shift = 2**block
    for c in range(chips):
        for slot in range(slots):
            to = pl.ds(c * width + slot * part, part)
            if slot >= shift:
                earlier[to, :] = narrow[pl.ds(c * width + (slot - shift) * part, part), :]
            else:
                at = (c + core) * width + (slot - shift + slots) * part
                earlier[to, :] = padded[pl.ds(pl.multiple_of(at, part), part), :]
            if slot + shift < slots:
                after[to, :] = narrow[pl.ds(c * width + (slot + shift) * part, part), :]
            else:
                at = (c + core + 1) * width + (slot + shift - slots) * part
                after[to, :] = padded[pl.ds(pl.multiple_of(at, part), part), :]
    for t in tiles(chips * width):
        x = advance(x_in[t, :], earlier[t, :], narrow[t, :], after[t, :], taps.at[block], output[block])
        x_ref[t, :] = x
        narrow_ref[t, :] = project(
            x, gain[block + 1 : block + 2, :], bias[block + 1 : block + 2, :], proj[block + 1]
        )


def rest_kernel(chips, width, first, layers, x_in, narrow, partner, gain, bias, taps, output, proj, *refs):
    pieces, (padded, own, x_ref) = refs[:chips], refs[chips:]
    blocks = range(first, layers)
    rows = chips * width
    chip, core = position()
    load_partner(partner, padded, chips, width)
    pad = (own.shape[1] - rows) // 2
    for n, block in enumerate(blocks):
        for t in tiles(rows):
            size = t.stop - t.start
            if n == 0:
                x = x_in[t, :]
                middle = narrow[t, :]
                earlier = padded[pl.ds(pl.multiple_of(core * width + t.start, width), size), :]
                after = padded[pl.ds(pl.multiple_of((core + 1) * width + t.start, width), size), :]
            else:
                x = x_ref[t, :]
                shift = 2 ** (n - 1) * width
                held = own.at[n - 1]
                middle = held[pl.ds(pad + t.start, size), :]
                earlier = held[pl.ds(pad + t.start - shift, size), :]
                after = held[pl.ds(pad + t.start + shift, size), :]
            x = advance(x, earlier, middle, after, taps.at[block], output[block])
            x_ref[t, :] = x
            if block + 1 < layers:
                own[n, pl.ds(pad + t.start, size), :] = project(
                    x, gain[block + 1 : block + 2, :], bias[block + 1 : block + 2, :], proj[block + 1]
                )
        if block + 1 < layers:
            own[n, pl.ds(0, pad), :] = own[n, pl.ds(rows, pad), :]
            own[n, pl.ds(pad + rows, pad), :] = own[n, pl.ds(pad, pad), :]
    for k in range(chips):
        pieces[k][...] = x_ref[pl.ds(pl.multiple_of((chip ^ k) * width, width), width), :]


def collect_kernel(ways, slots, part, chunks, chunk, *refs):
    pieces, (result, sems) = refs[: len(ways)], refs[-2:]
    chip, _ = position()
    copies = [
        pltpu.make_async_copy(
            pieces[n].at[pl.ds(slot * part, part), :],
            result.at[slot, (chip ^ k) * chunks + chunk],
            sems.at[n, slot],
        )
        for n, k in enumerate(ways)
        for slot in range(slots)
    ]
    for copy in copies:
        copy.start()
    for copy in copies:
        copy.wait()


def estimate(rows, model, neck, blocks):
    return pl.CostEstimate(
        flops=2 * rows * blocks * (2 * model * neck + 3 * neck * neck),
        bytes_accessed=blocks * 2 * (2 * model * neck + 3 * neck * neck) + 8 * rows * model,
        transcendentals=0,
    )


def travel_order(chips):
    half = chips // 2
    far = sorted(range(max(2, half), chips), key=lambda k: (-(k >> 1), k))
    return list(range(2, half)), far, list(range(1, min(2, chips)))


def leave_order(chips):
    near, far, next_to = travel_order(chips)
    return far[:2] + near + far[2:] + next_to


def chunk_count(chips):
    return max(1, min(CHUNKS, DILATION_START // chips // 16))


def body(stream, norm_gain, norm_bias, proj_in, convolution_taps, output_projection):
    rows, model = stream.shape
    layers, neck = norm_gain.shape[0], proj_in.shape[2]
    peers = lax.axis_size("blk")
    chips = peers // CORES
    slots = rows // DILATION_START
    span = DILATION_START // chips
    chunks = chunk_count(chips)
    part = span // chunks
    width = slots * part
    count = chips * width
    bf16 = jnp.bfloat16
    chip = lax.axis_index("blk") // CORES

    def to_chip(piece, k):
        return lax.ppermute(piece, "blk", [(i, i ^ (k * CORES)) for i in range(peers)])

    def other_core(narrow):
        return lax.ppermute(narrow, "blk", [(i, i ^ 1) for i in range(peers)])

    shape = jax.ShapeDtypeStruct
    load = pl.pallas_call(
        load_kernel,
        out_shape=shape((8, 128), jnp.float32),
        in_specs=[VMEM] * 3,
        out_specs=VMEM,
        compiler_params=LIMIT,
        name="load",
    )
    enter = pl.pallas_call(
        functools.partial(enter_kernel, chips, width),
        out_shape=(shape((count, model), bf16), shape((count, neck), bf16)),
        in_specs=[VMEM] * (chips + 4),
        out_specs=(VMEM, VMEM),
        cost_estimate=estimate(count, model, neck, 1),
        compiler_params=LIMIT,
        name="enter",
    )
    slot_block = pl.pallas_call(
        functools.partial(slot_kernel, chips, width, slots, 0),
        out_shape=(shape((count, model), bf16), shape((count, neck), bf16)),
        in_specs=[VMEM] * 8,
        out_specs=(VMEM, VMEM),
        scratch_shapes=[
            pltpu.VMEM((count + 2 * width, neck), bf16),
            pltpu.VMEM((count, neck), bf16),
            pltpu.VMEM((count, neck), bf16),
        ],
        cost_estimate=estimate(count, model, neck, 1),
        compiler_params=LIMIT,
        name="slot_block",
    )
    held = layers - 1
    pad = 2 ** (held - 2) * width
    rest = pl.pallas_call(
        functools.partial(rest_kernel, chips, width, 1, layers),
        out_shape=tuple(shape((width, model), bf16) for _ in range(chips)),
        in_specs=[VMEM] * 8,
        out_specs=tuple(VMEM for _ in range(chips)),
        scratch_shapes=[
            pltpu.VMEM((count + 2 * width, neck), bf16),
            pltpu.VMEM((held - 1, count + 2 * pad, neck), bf16),
            pltpu.VMEM((count, model), bf16),
        ],
        cost_estimate=estimate(count, model, neck, held),
        compiler_params=LIMIT,
        name="rest",
    )

    grid = stream.reshape(slots, chips * chunks, part, model)
    arrived = []
    for j in range(chunks):
        pieces = {}
        grid = lax.optimization_barrier(grid)
        for n, k in enumerate([*leave_order(chips), 0]):
            if j == 0 and n == 2:
                grid = lax.optimization_barrier(grid)
            piece = lax.dynamic_slice_in_dim(grid, (chip ^ k) * chunks + j, 1, axis=1).reshape(width, model)
            pieces[k] = to_chip(piece, k) if k else piece
        arrived.append([pieces[k] for k in range(chips)])

    weights = (norm_gain, norm_bias, convolution_taps, output_projection, proj_in)
    token = load(convolution_taps, output_projection, proj_in)
    left = []
    for j in range(chunks):
        x, narrow = enter(*arrived[j], norm_gain, norm_bias, proj_in, token)
        partner = other_core(narrow)
        x, narrow = slot_block(x, narrow, partner, *weights)
        partner = other_core(narrow)
        pieces = rest(x, narrow, partner, *weights)
        gone = {0: pieces[0]}
        for k in leave_order(chips):
            gone[k] = to_chip(pieces[k], k)
        left.append(gone)

    result = None
    leave = [0, *leave_order(chips)]
    late = travel_order(chips)[1][2:]
    groups = [(j, leave) for j in range(chunks - 1)]
    groups.append((chunks - 1, [k for k in leave if k not in late]))
    for n, (j, ways) in enumerate(groups):
        collect = pl.pallas_call(
            functools.partial(collect_kernel, ways, slots, part, chunks, j),
            out_shape=shape(grid.shape, bf16),
            in_specs=[VMEM] * len(ways) + [pl.BlockSpec(memory_space=pl.ANY)] * (n > 0),
            out_specs=pl.BlockSpec(memory_space=pl.ANY),
            scratch_shapes=[pltpu.SemaphoreType.DMA((len(ways), slots))],
            input_output_aliases={len(ways): 0} if n else {},
            compiler_params=LIMIT,
            name="collect",
        )
        result = collect(*[left[j][k] for k in ways], *([result] if n else []))
    for k in late:
        piece = left[-1][k].reshape(slots, 1, part, model)
        result = lax.dynamic_update_slice_in_dim(result, piece, (chip ^ k) * chunks + chunks - 1, axis=1)
    return result.reshape(rows, model)


def solution(mesh):
    return jax.shard_map(
        body,
        mesh=mesh,
        in_specs=(P(("batch", "blk"), None), P(), P(), P(), P(), P()),
        out_specs=P(("batch", "blk"), None),
        check_vma=False,
    )
```

```python
import functools

import jax
import jax.numpy as jnp
from jax import lax
from jax.experimental import pallas as pl
from jax.experimental.pallas import tpu as pltpu
from jax.sharding import PartitionSpec as P


DILATION_START = 512
EPSILON = 1e-05
CORES = 2
CHUNKS = 2
TILE = 512


VMEM = pl.BlockSpec(memory_space=pltpu.VMEM)
LIMIT = pltpu.CompilerParams(vmem_limit_bytes=12 << 20)


def gelu(x):
    return 0.5 * x * (1.0 + lax.erf(x * (0.5**0.5)))


def project(x, gain, bias, proj):
    values = x.astype(jnp.float32)
    average = jnp.mean(values, axis=1, keepdims=True)
    centred = values - average
    variance = jnp.mean(centred * centred, axis=1, keepdims=True)
    normed = (centred * lax.rsqrt(variance + EPSILON) * gain + bias).astype(jnp.bfloat16)
    return jnp.dot(normed, proj, preferred_element_type=jnp.float32).astype(jnp.bfloat16)


def advance(x, earlier, middle, after, taps, output):
    convolved = jnp.dot(middle, taps[1], preferred_element_type=jnp.float32)
    convolved = convolved + jnp.dot(earlier, taps[0], preferred_element_type=jnp.float32)
    convolved = convolved + jnp.dot(after, taps[2], preferred_element_type=jnp.float32)
    activated = gelu(convolved).astype(jnp.bfloat16)
    update = jnp.dot(activated, output, preferred_element_type=jnp.float32)
    return (x.astype(jnp.float32) + update).astype(jnp.bfloat16)


def tiles(rows):
    size = min(TILE, rows)
    return [slice(r, r + size) for r in range(0, rows, size)]


def position():
    index = lax.axis_index("blk")
    return index // CORES, index % CORES


def load_kernel(taps, output, proj, token):
    token[...] = jnp.zeros_like(token)


def enter_kernel(chips, width, *refs):
    pieces, (gain, bias, proj, _, x_ref, narrow_ref) = refs[:chips], refs[chips:]
    chip, _ = position()
    for k in range(chips):
        x_ref[pl.ds(pl.multiple_of((chip ^ k) * width, width), width), :] = pieces[k][...]
    for t in tiles(chips * width):
        narrow_ref[t, :] = project(x_ref[t, :], gain[0:1, :], bias[0:1, :], proj[0])


def load_partner(partner, padded, chips, width):
    rows = chips * width
    padded[pl.ds(width, rows), :] = partner[...]
    padded[pl.ds(0, width), :] = partner[pl.ds(rows - width, width), :]
    padded[pl.ds(width + rows, width), :] = partner[pl.ds(0, width), :]


def slot_kernel(chips, width, slots, block, x_in, narrow, partner, gain, bias, taps, output, proj,
                x_ref, narrow_ref, padded, earlier, after):
    _, core = position()
    load_partner(partner, padded, chips, width)
    part = width // slots
    shift = 2**block
    for c in range(chips):
        for slot in range(slots):
            to = pl.ds(c * width + slot * part, part)
            if slot >= shift:
                earlier[to, :] = narrow[pl.ds(c * width + (slot - shift) * part, part), :]
            else:
                at = (c + core) * width + (slot - shift + slots) * part
                earlier[to, :] = padded[pl.ds(pl.multiple_of(at, part), part), :]
            if slot + shift < slots:
                after[to, :] = narrow[pl.ds(c * width + (slot + shift) * part, part), :]
            else:
                at = (c + core + 1) * width + (slot + shift - slots) * part
                after[to, :] = padded[pl.ds(pl.multiple_of(at, part), part), :]
    for t in tiles(chips * width):
        x = advance(x_in[t, :], earlier[t, :], narrow[t, :], after[t, :], taps.at[block], output[block])
        x_ref[t, :] = x
        narrow_ref[t, :] = project(
            x, gain[block + 1 : block + 2, :], bias[block + 1 : block + 2, :], proj[block + 1]
        )


def rest_kernel(chips, width, first, layers, x_in, narrow, partner, gain, bias, taps, output, proj, *refs):
    pieces, (padded, own, x_ref) = refs[:chips], refs[chips:]
    blocks = range(first, layers)
    rows = chips * width
    chip, core = position()
    load_partner(partner, padded, chips, width)
    pad = (own.shape[1] - rows) // 2
    for n, block in enumerate(blocks):
        for t in tiles(rows):
            size = t.stop - t.start
            if n == 0:
                x = x_in[t, :]
                middle = narrow[t, :]
                earlier = padded[pl.ds(pl.multiple_of(core * width + t.start, width), size), :]
                after = padded[pl.ds(pl.multiple_of((core + 1) * width + t.start, width), size), :]
            else:
                x = x_ref[t, :]
                shift = 2 ** (n - 1) * width
                held = own.at[n - 1]
                middle = held[pl.ds(pad + t.start, size), :]
                earlier = held[pl.ds(pad + t.start - shift, size), :]
                after = held[pl.ds(pad + t.start + shift, size), :]
            x = advance(x, earlier, middle, after, taps.at[block], output[block])
            x_ref[t, :] = x
            if block + 1 < layers:
                own[n, pl.ds(pad + t.start, size), :] = project(
                    x, gain[block + 1 : block + 2, :], bias[block + 1 : block + 2, :], proj[block + 1]
                )
        if block + 1 < layers:
            own[n, pl.ds(0, pad), :] = own[n, pl.ds(rows, pad), :]
            own[n, pl.ds(pad + rows, pad), :] = own[n, pl.ds(pad, pad), :]
    for k in range(chips):
        pieces[k][...] = x_ref[pl.ds(pl.multiple_of((chip ^ k) * width, width), width), :]


def collect_kernel(ways, slots, part, chunks, chunk, *refs):
    pieces, (result, sems) = refs[: len(ways)], refs[-2:]
    chip, _ = position()
    copies = [
        pltpu.make_async_copy(
            pieces[n].at[pl.ds(slot * part, part), :],
            result.at[slot, (chip ^ k) * chunks + chunk],
            sems.at[n, slot],
        )
        for n, k in enumerate(ways)
        for slot in range(slots)
    ]
    for copy in copies:
        copy.start()
    for copy in copies:
        copy.wait()


def estimate(rows, model, neck, blocks):
    return pl.CostEstimate(
        flops=2 * rows * blocks * (2 * model * neck + 3 * neck * neck),
        bytes_accessed=blocks * 2 * (2 * model * neck + 3 * neck * neck) + 8 * rows * model,
        transcendentals=0,
    )


def travel_order(chips):
    half = chips // 2
    far = sorted(range(max(2, half), chips), key=lambda k: (-(k >> 1), k))
    return list(range(2, half)), far, list(range(1, min(2, chips)))


def arrive_order(chips):
    near, far, next_to = travel_order(chips)
    return far[:2] + near + far[2:] + next_to


def leave_order(chips):
    near, far, next_to = travel_order(chips)
    return far + near + next_to


def chunk_count(chips):
    return max(1, min(CHUNKS, DILATION_START // chips // 16))


def body(stream, norm_gain, norm_bias, proj_in, convolution_taps, output_projection):
    rows, model = stream.shape
    layers, neck = norm_gain.shape[0], proj_in.shape[2]
    peers = lax.axis_size("blk")
    chips = peers // CORES
    slots = rows // DILATION_START
    span = DILATION_START // chips
    chunks = chunk_count(chips)
    part = span // chunks
    width = slots * part
    count = chips * width
    bf16 = jnp.bfloat16
    chip = lax.axis_index("blk") // CORES

    def to_chip(piece, k):
        return lax.ppermute(piece, "blk", [(i, i ^ (k * CORES)) for i in range(peers)])

    def other_core(narrow):
        return lax.ppermute(narrow, "blk", [(i, i ^ 1) for i in range(peers)])

    shape = jax.ShapeDtypeStruct
    load = pl.pallas_call(
        load_kernel,
        out_shape=shape((8, 128), jnp.float32),
        in_specs=[VMEM] * 3,
        out_specs=VMEM,
        compiler_params=LIMIT,
        name="load",
    )
    enter = pl.pallas_call(
        functools.partial(enter_kernel, chips, width),
        out_shape=(shape((count, model), bf16), shape((count, neck), bf16)),
        in_specs=[VMEM] * (chips + 4),
        out_specs=(VMEM, VMEM),
        cost_estimate=estimate(count, model, neck, 1),
        compiler_params=LIMIT,
        name="enter",
    )
    slot_block = pl.pallas_call(
        functools.partial(slot_kernel, chips, width, slots, 0),
        out_shape=(shape((count, model), bf16), shape((count, neck), bf16)),
        in_specs=[VMEM] * 8,
        out_specs=(VMEM, VMEM),
        scratch_shapes=[
            pltpu.VMEM((count + 2 * width, neck), bf16),
            pltpu.VMEM((count, neck), bf16),
            pltpu.VMEM((count, neck), bf16),
        ],
        cost_estimate=estimate(count, model, neck, 1),
        compiler_params=LIMIT,
        name="slot_block",
    )
    held = layers - 1
    pad = 2 ** (held - 2) * width
    rest = pl.pallas_call(
        functools.partial(rest_kernel, chips, width, 1, layers),
        out_shape=tuple(shape((width, model), bf16) for _ in range(chips)),
        in_specs=[VMEM] * 8,
        out_specs=tuple(VMEM for _ in range(chips)),
        scratch_shapes=[
            pltpu.VMEM((count + 2 * width, neck), bf16),
            pltpu.VMEM((held - 1, count + 2 * pad, neck), bf16),
            pltpu.VMEM((count, model), bf16),
        ],
        cost_estimate=estimate(count, model, neck, held),
        compiler_params=LIMIT,
        name="rest",
    )

    grid = stream.reshape(slots, chips * chunks, part, model)
    arrived = []
    for j in range(chunks):
        pieces = {}
        grid = lax.optimization_barrier(grid)
        for k in [*arrive_order(chips), 0]:
            piece = lax.dynamic_slice_in_dim(grid, (chip ^ k) * chunks + j, 1, axis=1).reshape(width, model)
            pieces[k] = to_chip(piece, k) if k else piece
        arrived.append([pieces[k] for k in range(chips)])

    weights = (norm_gain, norm_bias, convolution_taps, output_projection, proj_in)
    token = load(convolution_taps, output_projection, proj_in)
    left = []
    for j in range(chunks):
        x, narrow = enter(*arrived[j], norm_gain, norm_bias, proj_in, token)
        partner = other_core(narrow)
        x, narrow = slot_block(x, narrow, partner, *weights)
        partner = other_core(narrow)
        pieces = rest(x, narrow, partner, *weights)
        gone = {0: pieces[0]}
        for k in leave_order(chips):
            gone[k] = to_chip(pieces[k], k)
        left.append(gone)

    result = None
    leave = [0, *leave_order(chips)]
    late = travel_order(chips)[1][2:]
    groups = [(j, leave) for j in range(chunks - 1)]
    groups.append((chunks - 1, [k for k in leave if k not in late]))
    for n, (j, ways) in enumerate(groups):
        collect = pl.pallas_call(
            functools.partial(collect_kernel, ways, slots, part, chunks, j),
            out_shape=shape(grid.shape, bf16),
            in_specs=[VMEM] * len(ways) + [pl.BlockSpec(memory_space=pl.ANY)] * (n > 0),
            out_specs=pl.BlockSpec(memory_space=pl.ANY),
            scratch_shapes=[pltpu.SemaphoreType.DMA((len(ways), slots))],
            input_output_aliases={len(ways): 0} if n else {},
            compiler_params=LIMIT,
            name="collect",
        )
        result = collect(*[left[j][k] for k in ways], *([result] if n else []))
    for k in late:
        piece = left[-1][k].reshape(slots, 1, part, model)
        result = lax.dynamic_update_slice_in_dim(result, piece, (chip ^ k) * chunks + chunks - 1, axis=1)
    return result.reshape(rows, model)


def solution(mesh):
    return jax.shard_map(
        body,
        mesh=mesh,
        in_specs=(P(("batch", "blk"), None), P(), P(), P(), P(), P()),
        out_specs=P(("batch", "blk"), None),
        check_vma=False,
    )
```
